32 devices in a mesh: dp: 8 (over z, core), seq: 4 (over y, x).
Axes of the slice: x: 2, y: 2, z: 4, core: 2. Of those that a mesh axis runs over, the one named last changes fastest.
Arguments:
- tokens: bfloat16 [8, 512, 576], P('dp', 'seq'), may hold values from -8 to 8
- weights: bfloat16 [1, 27648, 128], P(None, ('dp', 'seq')), may hold values from -0.2951389 to 0.2951389
- gains: bfloat16 [1152], P('seq'), may hold values from 0.25 to 1.75
- positions: int32 [8, 512], P('dp', 'seq'), may hold values from 0 to 511, each once within a row
- cotangent: bfloat16 [8, 512, 576], P('dp', 'seq'), may hold values from -6 to 6
Outputs:
- output_acts: float32 [8, 512, 576], P('dp', 'seq')
- input_grad: float32 [8, 512, 576], P('dp', 'seq')
- weight_grads: float32 [1, 27648, 128], P(None, ('dp', 'seq'))
- gain_grads: float32 [1152], P('seq')
The draws below stay inside these ranges and needn't reach their ends.
Inputs may be any that keep to these rules, and one draw needn't show every extreme that they name: Each sequence's positions are a permutation of 0 .. 511.
All inputs are finite; a program needn't handle non-finite values.
Results may differ from the reference program's by a relative error of at most 0.017.
Values may be sent and summed in bfloat16 or wider, within the bound.
No kernel may reach another device: no remote copies, remote signals or barrier semaphores. Data moves between devices by JAX's collectives and lax.ppermute only.
A program may use at most 128 MiB of HBM per device.

```python
import math
import jax
import jax.numpy as jnp
from jax import lax

D = 576
HQ = 9
HK = 3
HD = 64
FF = 1536
LANES = 128
LAYERS = 1
TOK_DEV = 128
SEQUENCES = 8
LENGTH = 512
PARAMS = 3538944


def draw_weights(key, part):
    own_key = jax.random.fold_in(key, 101)
    sample = jnp.clip(jax.random.normal(own_key, (LAYERS, PARAMS), jnp.float32), -6.0, 6.0) * (1.0 / math.sqrt(D))
    return sample.reshape(LAYERS, PARAMS // LANES, LANES).astype(jnp.bfloat16)


def draw_tokens(key, part):
    own_key = jax.random.fold_in(key, 202)
    sample = jnp.clip(jax.random.normal(own_key, (SEQUENCES, LENGTH, D), jnp.float32), -6.0, 6.0)
    return sample.astype(jnp.bfloat16)


def shard_levels(stream_key, extent, pieces, smallest, top_value):
    factor_of = 1.0
    for axis_at, blocks in pieces:
        draws = jax.random.uniform(jax.random.fold_in(jax.random.fold_in(stream_key, 6), axis_at), (blocks,), jnp.float32, smallest / len(pieces), top_value / len(pieces))
        factor_of = factor_of * jnp.repeat(jnp.exp(draws), extent[axis_at] // blocks).reshape((-1,) + (1,) * (len(extent) - 1 - axis_at))
    return factor_of


def centred(key, dims, scale, limit, shards=(), dtype=jnp.bfloat16):
    drawn = jax.random.normal(key, dims, jnp.float32) * scale
    if len(shards) > 0:
        drawn = shard_levels(key, dims, shards, -0.22, 0.18) * drawn
    return jnp.clip(drawn, min=-limit, max=limit).astype(dtype)


def setup_inputs(seed: int = 0) -> dict:
    key_list = jax.random.split(jax.random.key(seed), 6)
    return {
        "tokens": draw_tokens(jax.random.fold_in(key_list[5], 71), 0),
        "weights": draw_weights(jax.random.fold_in(key_list[5], 71), 0),
        "gains": jnp.clip(1.0 + 0.15 * jax.random.normal(key_list[2], (2 * LAYERS * D,), jnp.float32), 0.25, 1.75).astype(jnp.bfloat16),
        "positions": jax.vmap(lambda own: jax.random.permutation(own, LENGTH))(jax.random.split(key_list[3], SEQUENCES)).reshape((SEQUENCES, LENGTH)).astype(jnp.int32),
        "cotangent": centred(key_list[4], (SEQUENCES, LENGTH, D), 1.0, 6.0, ((0, 8), (1, 4))),
    }


EPSILON = 1e-05
THETA_BASE = 100000.0
MASKED = -1e+30

def unpack(table):
    q_width = HQ * HD
    k_width = HK * HD
    shapes = [(D, q_width), (D, k_width), (D, k_width), (q_width, D), (D, FF), (D, FF), (FF, D)]
    matrices = []
    offset = 0
    for row_count, col_count in shapes:
        span = row_count * col_count // LANES
        matrices.append(table[offset:offset + span].reshape(row_count, col_count))
        offset = offset + span
    return matrices

def tables(places):
    half_width = HD // 2
    frequency = THETA_BASE ** (-(jnp.arange(half_width).astype(jnp.float32) * (2.0 / HD)))
    angles = places.astype(jnp.float32)[:, None] * frequency[None, :]
    cos_table = jnp.cos(angles)
    sin_table = jnp.sin(angles)
    return (jnp.concatenate([cos_table, cos_table], -1)[:, None, :], jnp.concatenate([sin_table, sin_table], -1)[:, None, :])

def rotate(values):
    half_width = values.shape[-1] // 2
    return jnp.concatenate([-values[..., half_width:], values[..., :half_width]], -1)

def rotate_back(values):
    half_width = values.shape[-1] // 2
    return jnp.concatenate([values[..., half_width:], -values[..., :half_width]], -1)

def apply_rope(values, cos_table, sin_table):
    return values * cos_table + rotate(values) * sin_table

def undo_rope(gradient, cos_table, sin_table):
    return gradient * cos_table + rotate_back(gradient * sin_table)

def normed(stream, gain):
    recip = lax.rsqrt(lax.optimization_barrier(jnp.mean(stream * stream, -1, keepdims=True)) + EPSILON)
    return (stream * recip * gain.astype(jnp.float32)[None, :], recip)

def norm_back(gradient, stream, recip, gain):
    unit = stream * recip
    gain_grad = lax.optimization_barrier(jnp.sum(gradient * unit, 0))
    scaled = gradient * gain.astype(jnp.float32)[None, :]
    return (recip * (scaled - unit * lax.optimization_barrier(jnp.mean(scaled * unit, -1, keepdims=True))), gain_grad)

def product(left, right):
    return jnp.dot(left, right, preferred_element_type=jnp.float32)

def inner_blocks(left, right):
    block_count = left.shape[0] // TOK_DEV
    left_blocks = left.reshape(block_count, TOK_DEV, left.shape[1]).astype(jnp.float32)
    right_blocks = right.reshape(block_count, TOK_DEV, right.shape[1]).astype(jnp.float32)
    partial_sums = jnp.einsum('btr,btc->brc', left_blocks, right_blocks).astype(jnp.bfloat16)
    partial_sums = lax.optimization_barrier(partial_sums)
    return lax.optimization_barrier(jnp.sum(partial_sums.astype(jnp.float32), 0))

def scores_of(q_rot, keys, visible):
    group_size = HQ // HK
    score_scale = 1.0 / math.sqrt(HD)
    queries = q_rot.reshape(q_rot.shape[0], HK, group_size, HD).astype(jnp.float32)
    scores = jnp.einsum('qkgd,pkd->kgqp', queries, keys.astype(jnp.float32)) * score_scale
    return (jnp.where(visible[None, None], scores, MASKED), queries)

def attend(q_rot, keys, values, visible):
    scores, queries = scores_of(q_rot, keys, visible)
    row_max = lax.optimization_barrier(jnp.max(scores, -1, keepdims=True))
    log_total = row_max + jnp.log(lax.optimization_barrier(jnp.sum(jnp.exp(scores - row_max), -1, keepdims=True)))
    probs_low = jnp.exp(scores - log_total).astype(jnp.bfloat16)
    mixed = jnp.einsum('kgqp,pkd->qkgd', probs_low.astype(jnp.float32), values.astype(jnp.float32))
    return (mixed.reshape(q_rot.shape[0], HQ * HD).astype(jnp.bfloat16), log_total)

def attend_back(dmix_low, q_rot, keys, values, visible, log_total):
    group_size = HQ // HK
    score_scale = 1.0 / math.sqrt(HD)
    scores, queries = scores_of(q_rot, keys, visible)
    probs = jnp.exp(scores - log_total)
    probs_low = probs.astype(jnp.bfloat16)
    dmix = dmix_low.reshape(q_rot.shape[0], HK, group_size, HD).astype(jnp.float32)
    dprobs = jnp.einsum('qkgd,pkd->kgqp', dmix, values.astype(jnp.float32))
    delta = lax.optimization_barrier(jnp.sum(probs * dprobs, -1, keepdims=True))
    dscores = (probs * (dprobs - delta) * score_scale).astype(jnp.bfloat16).astype(jnp.float32)
    dquery = jnp.einsum('kgqp,pkd->qkgd', dscores, keys.astype(jnp.float32)).reshape(q_rot.shape[0], HQ, HD)
    dkey = jnp.einsum('kgqp,qkgd->pkd', dscores, queries)
    dvalue = jnp.einsum('kgqp,qkgd->pkd', probs_low.astype(jnp.float32), dmix)
    return (dquery, dkey, dvalue)

def layer_forward(stream, matrices, gain_in, gain_mid, cos_table, sin_table, visible):
    w_query, w_key, w_value, w_out, w_gate, w_up, w_down = matrices
    token_count = stream.shape[0]
    normed_in, recip_in = normed(stream, gain_in)
    normed_in = normed_in.astype(jnp.bfloat16)
    q_rot = apply_rope(product(normed_in, w_query).reshape(token_count, HQ, HD), cos_table, sin_table).astype(jnp.bfloat16)
    keys = apply_rope(product(normed_in, w_key).reshape(token_count, HK, HD), cos_table, sin_table).astype(jnp.bfloat16)
    values = product(normed_in, w_value).astype(jnp.bfloat16).reshape(token_count, HK, HD)
    mixed, log_total = attend(q_rot, keys, values, visible)
    middle = stream + product(mixed, w_out)
    normed_mid, recip_mid = normed(middle, gain_mid)
    normed_mid = normed_mid.astype(jnp.bfloat16)
    gate = product(normed_mid, w_gate)
    upward = product(normed_mid, w_up)
    hidden = (jax.nn.silu(gate) * upward).astype(jnp.bfloat16)
    result = middle + product(hidden, w_down)
    saved = (stream, normed_in, recip_in, q_rot, keys, values, mixed, log_total, middle, normed_mid, recip_mid, gate, upward, hidden)
    return (result, saved)

def layer_backward(grad_out, saved, matrices, gain_in, gain_mid, cos_table, sin_table, visible):
    w_query, w_key, w_value, w_out, w_gate, w_up, w_down = matrices
    stream, normed_in, recip_in, q_rot, keys, values, mixed, log_total, middle, normed_mid, recip_mid, gate, upward, hidden = saved
    token_count = stream.shape[0]
    grad_low = grad_out.astype(jnp.bfloat16)
    grad_down = inner_blocks(hidden, grad_low)
    dhidden = product(grad_low, w_down.T)
    sigma = jax.nn.sigmoid(gate)
    d_gate = (dhidden * upward * sigma * (1.0 + gate * (1.0 - sigma))).astype(jnp.bfloat16)
    d_up = (dhidden * gate * sigma).astype(jnp.bfloat16)
    grad_gate = inner_blocks(normed_mid, d_gate)
    grad_up = inner_blocks(normed_mid, d_up)
    d_norm = product(d_gate, w_gate.T) + product(d_up, w_up.T)
    back_mid, gain_mid_grad = norm_back(d_norm, middle, recip_mid, gain_mid)
    grad_mid = grad_out + back_mid
    mid_low = grad_mid.astype(jnp.bfloat16)
    grad_outw = inner_blocks(mixed, mid_low)
    dmix_low = product(mid_low, w_out.T).astype(jnp.bfloat16)
    dquery, dkey, dvalue = attend_back(dmix_low, q_rot, keys, values, visible, log_total)
    dquery = undo_rope(dquery, cos_table, sin_table).astype(jnp.bfloat16).reshape(token_count, HQ * HD)
    dkey = undo_rope(dkey, cos_table, sin_table).astype(jnp.bfloat16).reshape(token_count, HK * HD)
    dvalue = dvalue.astype(jnp.bfloat16).reshape(token_count, HK * HD)
    grad_query = inner_blocks(normed_in, dquery)
    grad_key = inner_blocks(normed_in, dkey)
    grad_value = inner_blocks(normed_in, dvalue)
    d_in = product(dquery, w_query.T) + product(dkey, w_key.T) + product(dvalue, w_value.T)
    back_in, gain_in_grad = norm_back(d_in, stream, recip_in, gain_in)
    grad_stream = grad_mid + back_in
    flat_grad = jnp.concatenate([part.reshape(-1, LANES) for part in (grad_query, grad_key, grad_value, grad_outw, grad_gate, grad_up, grad_down)], 0)
    return (grad_stream, flat_grad, gain_in_grad, gain_mid_grad)

def reference(tokens, weights, gains, positions, cotangent):
    layer_count = weights.shape[0]
    width = tokens.shape[-1]
    layer_mats = [unpack(weights[index]) for index in range(layer_count)]

    def one_sequence(carry, items):
        grad_weights, grad_gains = carry
        sequence, cotan, places = items
        cos_table, sin_table = tables(places)
        visible = places[None, :] <= places[:, None]
        stream = sequence.astype(jnp.float32)
        saved_list = []
        for index in range(layer_count):
            gain_in = gains[2 * index * width:(2 * index + 1) * width]
            gain_mid = gains[(2 * index + 1) * width:(2 * index + 2) * width]
            stream, saved = layer_forward(stream, layer_mats[index], gain_in, gain_mid, cos_table, sin_table, visible)
            saved_list.append(saved)
        result = stream
        gradient = cotan.astype(jnp.float32)
        flats = [None] * layer_count
        gain_parts = [None] * (2 * layer_count)
        for index in reversed(range(layer_count)):
            gain_in = gains[2 * index * width:(2 * index + 1) * width]
            gain_mid = gains[(2 * index + 1) * width:(2 * index + 2) * width]
            gradient, flat_grad, gin, gmid = layer_backward(gradient, saved_list[index], layer_mats[index], gain_in, gain_mid, cos_table, sin_table, visible)
            flats[index] = flat_grad
            gain_parts[2 * index] = gin
            gain_parts[2 * index + 1] = gmid
        grad_weights = grad_weights + jnp.stack(flats)
        grad_gains = grad_gains + jnp.concatenate(gain_parts)
        return ((grad_weights, grad_gains), (result, gradient))
    start_carry = (jnp.zeros(weights.shape, jnp.float32), jnp.zeros(gains.shape, jnp.float32))
    (grad_weights, grad_gains), (output_acts, input_grad) = lax.scan(one_sequence, start_carry, (tokens, cotangent, positions))
    return (output_acts, input_grad, grad_weights, grad_gains)
```

```python
import math

import jax
import jax.numpy as jnp
from jax import lax
from jax.experimental import pallas as pl
from jax.experimental.pallas import tpu as pltpu
from jax.sharding import PartitionSpec as P


D = 576
HQ = 9
HK = 3
HD = 64
FF = 1536
LANES = 128
LAYERS = 1


EPSILON = 1e-05
THETA_BASE = 100000.0
MASKED = -1e30


def unpack(table):
    q_width = HQ * HD
    k_width = HK * HD
    shapes = [(D, q_width), (D, k_width), (D, k_width), (q_width, D), (D, FF), (D, FF), (FF, D)]
    matrices = []
    offset = 0
    for row_count, col_count in shapes:
        span = row_count * col_count // LANES
        matrices.append(table[offset : offset + span].reshape(row_count, col_count))
        offset = offset + span
    return matrices


def tables(places):
    half_width = HD // 2
    frequency = THETA_BASE ** (-(jnp.arange(half_width).astype(jnp.float32) * (2.0 / HD)))
    angles = places.astype(jnp.float32)[:, None] * frequency[None, :]
    cos_table = jnp.cos(angles)
    sin_table = jnp.sin(angles)
    return (
        jnp.concatenate([cos_table, cos_table], -1),
        jnp.concatenate([sin_table, sin_table], -1),
    )


def first_halves(width):
    return jnp.arange(width) % HD < HD // 2


def rotate_flat(values):
    upper = first_halves(values.shape[-1])[None, :]
    return jnp.where(
        upper, -jnp.roll(values, -(HD // 2), axis=-1), jnp.roll(values, HD // 2, axis=-1)
    )


def rotate_back_flat(values):
    upper = first_halves(values.shape[-1])[None, :]
    return jnp.where(
        upper, jnp.roll(values, -(HD // 2), axis=-1), -jnp.roll(values, HD // 2, axis=-1)
    )


def apply_rope(values, cos_wide, sin_wide):
    return values * cos_wide + rotate_flat(values) * sin_wide


def undo_rope(gradient, cos_wide, sin_wide):
    return gradient * cos_wide + rotate_back_flat(gradient * sin_wide)


def normed(stream, gain):
    recip = lax.rsqrt(jnp.mean(stream * stream, -1, keepdims=True) + EPSILON)
    return (stream * recip * gain.astype(jnp.float32)[None, :], recip)


def norm_back(gradient, stream, recip, gain):
    unit = stream * recip
    gain_grad = jnp.sum(gradient * unit, 0)
    scaled = gradient * gain.astype(jnp.float32)[None, :]
    return (recip * (scaled - unit * jnp.mean(scaled * unit, -1, keepdims=True)), gain_grad)


def product(left, right):
    return jnp.dot(left, right, preferred_element_type=jnp.float32)


def product_t(left, right):
    return lax.dot_general(
        left, right, (((1,), (1,)), ((), ())), preferred_element_type=jnp.float32
    )


def inner(left, right):
    return lax.dot_general(
        left, right, (((0,), (0,)), ((), ())), preferred_element_type=jnp.float32
    )


def query_heads(flat):
    group_size = HQ // HK
    return flat.T.reshape(HK, group_size, HD, flat.shape[0])


def heads_to_rows(heads):
    return heads.reshape(HQ * HD, heads.shape[-1]).T


def scores_of(q_heads, keys_t, visible):
    score_scale = 1.0 / math.sqrt(HD)
    scores = (
        jnp.einsum("kgdq,kdp->kgqp", q_heads, keys_t, preferred_element_type=jnp.float32)
        * score_scale
    )
    return jnp.where(visible[None, None], scores, MASKED)


def attend(q_heads, keys_t, values_t, visible):
    scores = scores_of(q_heads, keys_t, visible)
    row_max = jnp.max(scores, -1)
    log_total = row_max + jnp.log(jnp.sum(jnp.exp(scores - row_max[..., None]), -1))
    probs_low = jnp.exp(scores - log_total[..., None]).astype(jnp.bfloat16)
    mixed_t = jnp.einsum("kgqp,kdp->kgdq", probs_low, values_t, preferred_element_type=jnp.float32)
    return (heads_to_rows(mixed_t).astype(jnp.bfloat16), log_total)


def attend_back(dmix_low, q_heads, keys_t, values_t, visible, log_total):
    score_scale = 1.0 / math.sqrt(HD)
    scores = scores_of(q_heads, keys_t, visible)
    probs = jnp.exp(scores - log_total[..., None])
    probs_low = probs.astype(jnp.bfloat16)
    dmix = query_heads(dmix_low)
    dprobs = jnp.einsum("kgdq,kdp->kgqp", dmix, values_t, preferred_element_type=jnp.float32)
    delta = jnp.sum(probs * dprobs, -1, keepdims=True)
    dscores = (probs * (dprobs - delta) * score_scale).astype(jnp.bfloat16)
    dquery = heads_to_rows(
        jnp.einsum("kgqp,kdp->kgdq", dscores, keys_t, preferred_element_type=jnp.float32)
    )
    dkey_t = jnp.einsum("kgqp,kgdq->kdp", dscores, q_heads, preferred_element_type=jnp.float32)
    dvalue_t = jnp.einsum("kgqp,kgdq->kdp", probs_low, dmix, preferred_element_type=jnp.float32)
    return (dquery, dkey_t, dvalue_t)


def fetch(layer_shard):
    return unpack(lax.all_gather(layer_shard, ("dp", "seq"), axis=0, tiled=True))


def fetch_again(layer_shard):
    return unpack(lax.all_gather(layer_shard, ("dp", "seq"), axis=0, tiled=True))


def layer_forward(stream, matrices, gain_in, gain_mid, rope, visible):
    w_query, w_key, w_value, w_out, w_gate, w_up, w_down = matrices
    cos_query, sin_query, cos_key, sin_key = rope
    token_count = stream.shape[0]
    normed_in, recip_in = normed(stream, gain_in)
    normed_in = normed_in.astype(jnp.bfloat16)
    q_rot = apply_rope(product(normed_in, w_query), cos_query, sin_query).astype(jnp.bfloat16)
    q_heads = query_heads(q_rot)
    key_local = apply_rope(product(normed_in, w_key), cos_key, sin_key).astype(jnp.bfloat16)
    value_local = product(normed_in, w_value).astype(jnp.bfloat16)
    key_t = key_local.T.reshape(HK, HD, token_count)
    value_t = value_local.T.reshape(HK, HD, token_count)
    keys_t, values_t = (
        lax.all_gather(key_t, "seq", axis=2, tiled=True),
        lax.all_gather(value_t, "seq", axis=2, tiled=True),
    )
    mixed, log_total = attend(q_heads, keys_t, values_t, visible)
    middle = stream + product(mixed, w_out)
    normed_mid, recip_mid = normed(middle, gain_mid)
    normed_mid = normed_mid.astype(jnp.bfloat16)
    gate = product(normed_mid, w_gate)
    upward = product(normed_mid, w_up)
    hidden = (jax.nn.silu(gate) * upward).astype(jnp.bfloat16)
    result = middle + product(hidden, w_down)
    saved = (
        stream,
        normed_in,
        recip_in,
        q_heads,
        keys_t,
        values_t,
        mixed,
        log_total,
        middle,
        normed_mid,
        recip_mid,
        gate,
        upward,
        hidden,
    )
    return (result, saved)


def layer_backward(grad_out, saved, matrices, gain_in, gain_mid, rope, visible):
    w_query, w_key, w_value, w_out, w_gate, w_up, w_down = matrices
    cos_query, sin_query, cos_key, sin_key = rope
    (
        stream,
        normed_in,
        recip_in,
        q_heads,
        keys_t,
        values_t,
        mixed,
        log_total,
        middle,
        normed_mid,
        recip_mid,
        gate,
        upward,
        hidden,
    ) = saved
    token_count = stream.shape[0]
    grad_low = grad_out.astype(jnp.bfloat16)
    grad_down = inner(hidden, grad_low)
    dhidden = product_t(grad_low, w_down)
    sigma = jax.nn.sigmoid(gate)
    d_gate = (dhidden * upward * sigma * (1.0 + gate * (1.0 - sigma))).astype(jnp.bfloat16)
    d_up = (dhidden * gate * sigma).astype(jnp.bfloat16)
    grad_gate = inner(normed_mid, d_gate)
    grad_up = inner(normed_mid, d_up)
    d_norm = product_t(d_gate, w_gate) + product_t(d_up, w_up)
    back_mid, gain_mid_grad = norm_back(d_norm, middle, recip_mid, gain_mid)
    grad_mid = grad_out + back_mid
    mid_low = grad_mid.astype(jnp.bfloat16)
    grad_outw = inner(mixed, mid_low)
    dmix_low = product_t(mid_low, w_out).astype(jnp.bfloat16)
    dquery, dkey_part, dvalue_part = attend_back(
        dmix_low, q_heads, keys_t, values_t, visible, log_total
    )
    dkey_t, dvalue_t = (
        lax.psum_scatter(
            dkey_part.astype(jnp.bfloat16), "seq", scatter_dimension=2, tiled=True
        ).astype(jnp.float32),
        lax.psum_scatter(
            dvalue_part.astype(jnp.bfloat16), "seq", scatter_dimension=2, tiled=True
        ).astype(jnp.float32),
    )
    dquery = undo_rope(dquery, cos_query, sin_query).astype(jnp.bfloat16)
    dkey = undo_rope(dkey_t.reshape(HK * HD, token_count).T, cos_key, sin_key).astype(jnp.bfloat16)
    dvalue = dvalue_t.reshape(HK * HD, token_count).T.astype(jnp.bfloat16)
    grad_query = inner(normed_in, dquery)
    grad_key = inner(normed_in, dkey)
    grad_value = inner(normed_in, dvalue)
    d_in = product_t(dquery, w_query) + product_t(dkey, w_key) + product_t(dvalue, w_value)
    back_in, gain_in_grad = norm_back(d_in, stream, recip_in, gain_in)
    grad_stream = grad_mid + back_in
    flat_grad = jnp.concatenate(
        [
            part.reshape(-1, LANES)
            for part in (grad_query, grad_key, grad_value, grad_outw, grad_gate, grad_up, grad_down)
        ],
        0,
    )
    return (grad_stream, flat_grad, gain_in_grad, gain_mid_grad)


def shards(tokens, weights, gains, positions, cotangent):
    places = positions[0]
    key_places = lax.all_gather(places, "seq", axis=0, tiled=True)
    visible = key_places[None, :] <= places[:, None]
    cos_head, sin_head = tables(places)
    rope = (
        jnp.tile(cos_head, (1, HQ)),
        jnp.tile(sin_head, (1, HQ)),
        jnp.tile(cos_head, (1, HK)),
        jnp.tile(sin_head, (1, HK)),
    )
    gain_full = lax.all_gather(gains, "seq", axis=0, tiled=True)
    stream = tokens[0].astype(jnp.float32)
    layer_index = 0
    matrices = fetch(weights[layer_index])
    gain_in = gain_full[2 * layer_index * D : (2 * layer_index + 1) * D]
    gain_mid = gain_full[(2 * layer_index + 1) * D : (2 * layer_index + 2) * D]
    stream, saved = layer_forward(stream, matrices, gain_in, gain_mid, rope, visible)
    saved_list = [saved]
    gradient = cotangent[0].astype(jnp.float32)
    flats = [None] * LAYERS
    gain_parts = [None] * (2 * LAYERS)
    for layer_index in reversed(range(LAYERS)):
        matrices = fetch_again(weights[layer_index])
        gain_in = gain_full[2 * layer_index * D : (2 * layer_index + 1) * D]
        gain_mid = gain_full[(2 * layer_index + 1) * D : (2 * layer_index + 2) * D]
        gradient, flat_grad, gin, gmid = layer_backward(
            gradient, saved_list[layer_index], matrices, gain_in, gain_mid, rope, visible
        )
        flats[layer_index] = flat_grad
        gain_parts[2 * layer_index] = gin
        gain_parts[2 * layer_index + 1] = gmid
    dp_count = lax.axis_size("dp")
    seq_count = lax.axis_size("seq")
    stacked = jnp.stack(flats)
    row_share = stacked.shape[1] // (dp_count * seq_count)
    arranged = stacked.reshape(LAYERS, dp_count, seq_count, row_share, LANES).transpose(
        2, 0, 1, 3, 4
    )
    arranged = arranged.reshape(seq_count * LAYERS * dp_count * row_share, LANES)
    seq_total = lax.psum_scatter(
        arranged.astype(jnp.bfloat16), "seq", scatter_dimension=0, tiled=True
    ).astype(jnp.float32)
    weight_share = lax.psum_scatter(
        seq_total.reshape(LAYERS, dp_count * row_share, LANES).astype(jnp.bfloat16),
        "dp",
        scatter_dimension=1,
        tiled=True,
    ).astype(jnp.float32)
    gain_total = lax.psum(jnp.concatenate(gain_parts), ("dp", "seq"))
    gain_piece = gain_total.shape[0] // seq_count
    gain_share = lax.dynamic_slice_in_dim(
        gain_total, lax.axis_index("seq") * gain_piece, gain_piece
    )
    return (stream[None], gradient[None], weight_share, gain_share)


PIECE = 864
EXTRA = 16
F32 = jnp.float32
BF16 = jnp.bfloat16
PAD = 640
TOK = 128
ROOM = 24 * 1024 * 1024


def any_spec():
    return pl.BlockSpec(memory_space=pl.ANY)


def vmem_spec():
    return pl.BlockSpec(memory_space=pltpu.VMEM)


def shape(dims, dtype):
    return jax.ShapeDtypeStruct(dims, dtype)


def swap_halves(block):
    return pltpu.roll(block, 64, 1)


def low_lanes(block):
    return lax.broadcasted_iota(jnp.int32, block.shape, 1) < 64


def dot_nn(left, right):
    return lax.dot_general(left, right, (((1,), (0,)), ((), ())), preferred_element_type=F32)


def dot_nt(left, right):
    return lax.dot_general(left, right, (((1,), (1,)), ((), ())), preferred_element_type=F32)


def dot_tn(left, right):
    return lax.dot_general(left, right, (((0,), (0,)), ((), ())), preferred_element_type=F32)


def widen(value):
    rows = value.shape[0]
    return jnp.concatenate([value, jnp.zeros((rows, PAD - value.shape[1]), value.dtype)], 1)


def split_rows(value):
    high = value.astype(BF16)
    return jnp.concatenate([high, (value - high.astype(F32)).astype(BF16)], 0)


def unsplit(ref, row):
    return ref[row : row + 16, :].astype(F32) + ref[row + 16 : row + 32, :].astype(F32)


def coordinates():
    dp_index = lax.axis_index("dp")
    place = lax.axis_index("seq")
    z = dp_index // 2
    piece_index = dp_index * 4 + place
    narrow_piece = (piece_index == 3) | (piece_index == 4)
    kind = jnp.where((z == 1) | (z == 2), 2, jnp.where(narrow_piece, 1, 0))
    return z, dp_index % 2, place, kind


def prep_kernel(w_ref, out_ref, rows, blocks, packed, wide):
    rows[...] = w_ref[...].astype(F32)
    kind = coordinates()[3]

    @pl.when(kind == 2)
    def _():
        for c in range(12):
            packed[c * 72 : (c + 1) * 72, :] = rows[pl.ds(c, 72, stride=12), :]

    @pl.when(kind == 0)
    def _():
        t = [rows[pl.ds(c, 96, stride=9), :] for c in range(9)]
        low = low_lanes(t[0])
        turned = [swap_halves(x) for x in t[4:]]
        for c in range(5):
            blocks.at[c][pl.ds(0, 96, stride=2), :] = t[c]
            odd = jnp.where(low, turned[c], turned[c + 1]) if c < 4 else turned[4]
            blocks.at[c][pl.ds(1, 96, stride=2), :] = odd
        for c in range(4):
            packed[c * 192 : (c + 1) * 192, :] = blocks[c]
        half = blocks[4]
        packed[768:864, :] = jnp.where(low, half[0:96], swap_halves(half[96:192]))

    @pl.when(kind == 1)
    def _():
        t = [rows[pl.ds(c, 288, stride=3), :] for c in range(3)]
        low = low_lanes(t[0])
        turned = [swap_halves(x) for x in t[1:]]
        wide.at[0][pl.ds(0, 288, stride=2), :] = t[0]
        wide.at[0][pl.ds(1, 288, stride=2), :] = jnp.where(low, turned[0], turned[1])
        wide.at[1][pl.ds(0, 288, stride=2), :] = t[1]
        wide.at[1][pl.ds(1, 288, stride=2), :] = turned[1]
        packed[0:576, :] = wide[0]
        half = wide[1]
        packed[576:864, :] = jnp.where(low, half[0:288], swap_halves(half[288:576]))

    out_ref[...] = packed[...].astype(BF16)


def prep(shard):
    return pl.pallas_call(
        prep_kernel,
        out_shape=shape((PIECE, LANES), BF16),
        in_specs=[vmem_spec()],
        out_specs=vmem_spec(),
        scratch_shapes=[
            pltpu.VMEM((PIECE, LANES), F32),
            pltpu.VMEM((5, 192, LANES), F32),
            pltpu.VMEM((PIECE, LANES), F32),
            pltpu.VMEM((2, 576, LANES), F32),
        ],
        name="prep",
        compiler_params=pltpu.CompilerParams(vmem_limit_bytes=ROOM),
    )(shard)


def extend_kernel(tok_ref, gain_ref, pos_ref, out_ref):
    out_ref[0:D, :] = tok_ref[...]
    gain = gain_ref[...].astype(F32)
    last = jnp.concatenate([gain[:, 256:288], jnp.zeros((1, 96), F32)], 1)
    place = pos_ref[...]
    extra = jnp.concatenate(
        [
            gain[:, 0:LANES],
            gain[:, LANES:256],
            last,
            (place // 64).astype(F32),
            (place % 64).astype(F32),
            jnp.zeros((EXTRA - 5, LANES), F32),
        ],
        0,
    )
    out_ref[D : D + EXTRA, :] = extra.astype(BF16)


def extend(tokens_t, gain_row, places):
    return pl.pallas_call(
        extend_kernel,
        out_shape=shape((D + EXTRA, LANES), BF16),
        in_specs=[vmem_spec()] * 3,
        out_specs=vmem_spec(),
        name="extend",
        compiler_params=pltpu.CompilerParams(vmem_limit_bytes=ROOM),
    )(tokens_t, gain_row, places)


def tables_kernel(
    e0, e1, e2, e3, freq_ref, gain_in, gain_mid, cos_ref, sin_ref, qpos_ref, kpos_ref, slots
):
    place = coordinates()[2]
    for j, ref in enumerate((e0, e1, e2, e3)):
        extra = ref[...].astype(F32)
        slots[lax.bitwise_xor(place, j)] = extra[0:8, :]
        row = extra[3:4, :] * 64.0 + extra[4:5, :]
        part = slice(j * TOK, (j + 1) * TOK)
        kpos_ref[:, part] = row
        column = jnp.broadcast_to(row, (8, LANES)).T[:, 0:1]
        if j == 0:
            qpos_ref[...] = column
        angles = column * freq_ref[...]
        cos_ref[part, :] = jnp.cos(angles)
        sin_ref[part, :] = jnp.sin(angles)
    lane = lax.broadcasted_iota(jnp.int32, (1, LANES), 1)
    for n, out in enumerate((gain_in, gain_mid)):
        first = slots[2 * n]
        second = pltpu.roll(slots[2 * n + 1], 32, 1)
        out[:, 0:128] = first[0:1]
        out[:, 128:256] = first[1:2]
        out[:, 256:384] = jnp.where(lane < 32, first[2:3], second[0:1])
        out[:, 384:512] = jnp.where(lane < 32, second[0:1], second[1:2])
        out[:, 512:576] = jnp.where(lane < 32, second[1:2], second[2:3])[:, 0:64]


def tables_of(toks, frequency):
    def block(index):
        return pl.BlockSpec((EXTRA, LANES), lambda i: (index, 0))

    def whole(rows, columns):
        return pl.BlockSpec((rows, columns), lambda i: (0, 0))

    outs = ((1, D), (1, D), (4 * TOK, LANES), (4 * TOK, LANES), (TOK, 1), (1, 4 * TOK))
    return pl.pallas_call(
        tables_kernel,
        grid=(1,),
        out_shape=tuple(shape(dims, F32) for dims in outs),
        in_specs=[block(36)] * 4 + [whole(1, LANES)],
        out_specs=tuple(whole(*dims) for dims in outs),
        scratch_shapes=[pltpu.VMEM((4, 8, LANES), F32)],
        name="tables",
        compiler_params=pltpu.CompilerParams(vmem_limit_bytes=ROOM),
    )(*toks, frequency)


def scales_kernel(own, got1, got2, got3, gain_out):
    place = coordinates()[2]
    gains = own[...] + got1[...] + got2[...] + got3[...]
    gains = jnp.where(place < 2, gains[0:5, :], gains[5:10, :])
    row = jnp.concatenate([gains[n : n + 1, :] for n in range(5)], 1)
    row = jnp.broadcast_to(row, (8, PAD))
    row = jnp.where(place % 2 == 0, row, pltpu.roll(row, PAD - 288, 1))
    gain_out[...] = row[0:1, 0:288]


def scales(parts):
    return pl.pallas_call(
        scales_kernel,
        out_shape=shape((1, 288), F32),
        in_specs=[vmem_spec()] * 4,
        out_specs=vmem_spec(),
        name="scales",
        compiler_params=pltpu.CompilerParams(vmem_limit_bytes=ROOM),
    )(*parts)


def finish_kernel(attn_ref, down_ref, inner_ref, *refs):
    _, out_ref, blocks, packed, wide = refs[9:]
    z, _, _, kind = coordinates()
    outer = jnp.where(z == 0, attn_ref[...], down_ref[...]).astype(F32)
    total = jnp.where((z == 0) | (z == 3), outer, inner_ref[...])
    for part in refs[:9]:
        total = total + part[...].astype(F32)
    packed[...] = total

    @pl.when(kind == 2)
    def _():
        for c in range(12):
            out_ref[pl.ds(c, 72, stride=12), :] = packed[c * 72 : (c + 1) * 72, :]

    @pl.when(kind == 0)
    def _():
        for c in range(4):
            blocks[c] = packed[c * 192 : (c + 1) * 192, :]
        half = packed[768:864, :]
        blocks.at[4][0:96, :] = half
        blocks.at[4][96:192, :] = swap_halves(half)
        low = low_lanes(half)
        even = [blocks.at[c][pl.ds(0, 96, stride=2), :] for c in range(5)]
        odd = [swap_halves(blocks.at[c][pl.ds(1, 96, stride=2), :]) for c in range(5)]
        for c in range(4):
            out_ref[pl.ds(c, 96, stride=9), :] = even[c]
            out_ref[pl.ds(c + 5, 96, stride=9), :] = jnp.where(low, odd[c], odd[c + 1])
        out_ref[pl.ds(4, 96, stride=9), :] = jnp.where(low, even[4], odd[0])

    @pl.when(kind == 1)
    def _():
        wide[0] = packed[0:576, :]
        half = packed[576:864, :]
        wide.at[1][0:288, :] = half
        wide.at[1][288:576, :] = swap_halves(half)
        low = low_lanes(half)
        even = [wide.at[c][pl.ds(0, 288, stride=2), :] for c in range(2)]
        odd = [swap_halves(wide.at[c][pl.ds(1, 288, stride=2), :]) for c in range(2)]
        out_ref[pl.ds(0, 288, stride=3), :] = even[0]
        out_ref[pl.ds(1, 288, stride=3), :] = jnp.where(low, even[1], odd[0])
        out_ref[pl.ds(2, 288, stride=3), :] = jnp.where(low, odd[0], odd[1])


def finish(attn, down, inner, parts, after):
    return pl.pallas_call(
        finish_kernel,
        out_shape=shape((PIECE, LANES), F32),
        in_specs=[vmem_spec()] * (3 + len(parts)) + [any_spec()],
        out_specs=vmem_spec(),
        scratch_shapes=[
            pltpu.VMEM((5, 192, LANES), F32),
            pltpu.VMEM((PIECE, LANES), F32),
            pltpu.VMEM((2, 576, LANES), F32),
        ],
        name="finish",
        compiler_params=pltpu.CompilerParams(vmem_limit_bytes=ROOM),
    )(attn, down, inner, *parts, after)


def split_kernel(beside, across, upper, lower):
    upper[...] = beside[0:CUT, :]
    lower[...] = across[CUT:PIECE, :]


def split(beside, across):
    return pl.pallas_call(
        split_kernel,
        out_shape=(shape((CUT, LANES), BF16), shape((PIECE - CUT, LANES), BF16)),
        in_specs=[vmem_spec()] * 2,
        out_specs=(vmem_spec(), vmem_spec()),
        name="split",
        compiler_params=pltpu.CompilerParams(vmem_limit_bytes=ROOM),
    )(beside, across)


def rows_at(start, size, align=8):
    return pl.ds(pl.multiple_of(start, align), size)


CUT = 432


def copies(arrays, j, blocks):
    if j < 3:
        return [(arrays[j], row, n, 0, count) for n, (row, count) in enumerate(blocks)]
    out = []
    for n, (row, count) in enumerate(blocks):
        if row < CUT:
            size = min(count, CUT - row)
            out.append((arrays[3], row, n, 0, size))
        if row + count > CUT:
            start = max(row, CUT)
            out.append((arrays[4], start - CUT, n, start - row, row + count - start))
    return out


def each_piece(meta, pair, body):
    for part, arrays in enumerate(pair):
        core = meta[1] if part == 0 else 1 - meta[1]
        for j in range(4):
            body(arrays, j, core, lax.bitwise_xor(meta[2], j))


def fetch_wide(meta, pair, matrix, sem):
    def one(arrays, j, core, place):
        target = rows_at((4 * core + place) * 72, 72)
        if j < 3:
            pltpu.make_async_copy(arrays[j], matrix.at[:, target, :], sem).start()
        else:
            pltpu.make_async_copy(arrays[3], matrix.at[0:6, target, :], sem).start()
            pltpu.make_async_copy(arrays[4], matrix.at[6:12, target, :], sem).start()

    each_piece(meta, pair, one)


def fetch_tall_piece(arrays, j, matrix, half, slot, sem, half_sem):
    blocks = [(c * 192, 192) for c in range(4)] + [(768, 96)]
    for array, row, n, offset, count in copies(arrays, j, blocks):
        if n < 4:
            target = matrix.at[rows_at(slot * 192 + offset, count), n * LANES : (n + 1) * LANES]
        else:
            target = half.at[rows_at(slot * 96 + offset, count), :]
        source = array.at[row : row + count, :]
        pltpu.make_async_copy(source, target, sem if n < 4 else half_sem).start()


def fetch_down(meta, pair, matrix, half, sem, half_sem):
    def one(arrays, j, core, place):
        fetch_tall_piece(arrays, j, matrix, half, 4 * core + place, sem, half_sem)

    each_piece(meta, pair, one)


def wait_all(ref, sem):
    pltpu.make_async_copy(ref, ref, sem).wait()


def place_halves(matrix, half, count):
    for n in range(count):
        block = half[n * 96 : (n + 1) * 96, :].astype(F32)
        matrix[n * 192 : n * 192 + 96, 512:PAD] = block.astype(BF16)
        matrix[n * 192 + 96 : (n + 1) * 192, 512:PAD] = swap_halves(block).astype(BF16)


def fetch_attention(meta, pair, matrix, half, narrow, narrow_half, sems):
    def one(arrays, j, core, place):
        is_narrow = jnp.where(core == 0, place == 3, place == 0)

        @pl.when(is_narrow)
        def _():
            for array, row, n, offset, count in copies(arrays, j, [(0, 576), (576, 288)]):
                if n == 0:
                    target = narrow.at[rows_at(core * 576 + offset, count), 0:LANES]
                else:
                    target = narrow_half.at[rows_at(core * 288 + offset, count), :]
                source = array.at[row : row + count, :]
                pltpu.make_async_copy(source, target, sems.at[2 + n]).start()

        @pl.when(jnp.logical_not(is_narrow))
        def _():
            slot = jnp.where(core == 0, place, place + 2)
            fetch_tall_piece(arrays, j, matrix, half, slot, sems.at[0], sems.at[1])

    each_piece(meta, pair, one)


def rope(block, cos, sin):
    first = lax.broadcasted_iota(jnp.int32, block.shape, 1) % HD < HD // 2
    turned = jnp.where(first, -pltpu.roll(block, 96, 1), pltpu.roll(block, 32, 1))
    return block * cos + turned * sin


def unrope(block, cos, sin):
    first = lax.broadcasted_iota(jnp.int32, block.shape, 1) % HD < HD // 2
    scaled = block * sin
    turned = jnp.where(first, pltpu.roll(scaled, 96, 1), -pltpu.roll(scaled, 32, 1))
    return block * cos + turned


def kv_of(ref, group):
    size = 4 * TOK
    keys = ref[group * size : (group + 1) * size, :]
    values = ref[(group + 3) * size : (group + 4) * size, :]
    return keys, values


def merge_heads(heads):
    low = low_lanes(heads[0])
    out = []
    for b in range(5):
        other = swap_halves(heads[2 * b + 1]) if b < 4 else jnp.zeros_like(heads[0])
        out.append(jnp.where(low, heads[2 * b], other))
    return jnp.concatenate(out, 1)


def pairs_of(refs):
    return [(refs[n : n + 5], refs[n + 5 : n + 10]) for n in range(0, len(refs), 10)]


def attend_kernel(*refs):
    pairs = pairs_of(refs[:30])
    (
        tok0, tok1, tok2, tok3, gain_ref, gain_mid_ref, cos_ref, sin_ref, qpos_ref, kpos_ref,
        q_ref, kv_ref, early_ref, matrix, narrow, total_ref, middle_ref,
        half, narrow_half, sems,
    ) = refs[30:]
    meta = coordinates()
    z = meta[0]
    targets = (matrix, half, narrow, narrow_half, sems)
    for test, pair in ((z == 0, pairs[0]), (z == 1, pairs[1]), (z >= 2, pairs[2])):

        @pl.when(test)
        def _():
            fetch_attention(meta, pair, *targets)

    gain = gain_ref[...]
    normed_all = []
    own_stream = None
    for ref in (tok0, tok1, tok2, tok3):
        stream = ref[0:D, :].astype(F32).T
        if own_stream is None:
            own_stream = stream
        recip = lax.rsqrt(jnp.mean(stream * stream, -1, keepdims=True) + EPSILON)
        normed_all.append((stream * recip * gain).astype(BF16))
    nin = normed_all[0]
    everyone = jnp.concatenate(normed_all, 0)
    early_ref[:, 0:PAD] = widen(nin)
    cos = cos_ref[...]
    sin = sin_ref[...]
    visible = kpos_ref[...] <= qpos_ref[...]
    visible = jnp.concatenate([visible] * 3, 0)
    wait_all(matrix.at[:, 0:512], sems.at[0])
    wait_all(half, sems.at[1])
    wait_all(narrow.at[:, 0:LANES], sems.at[2])
    wait_all(narrow_half, sems.at[3])
    place_halves(matrix, half, 6)
    for n in range(2):
        block = narrow_half[n * 288 : (n + 1) * 288, :].astype(F32)
        narrow[n * 576 : n * 576 + 288, LANES:256] = block.astype(BF16)
        narrow[n * 576 + 288 : (n + 1) * 576, LANES:256] = swap_halves(block).astype(BF16)
    query = dot_nn(nin, matrix[0:D, :])
    low = lax.broadcasted_iota(jnp.int32, (TOK, LANES), 1) < 64
    for b in range(5):
        block = rope(query[:, b * LANES : (b + 1) * LANES], cos[0:TOK], sin[0:TOK])
        q_ref[2 * b * TOK : (2 * b + 1) * TOK, :] = jnp.where(low, block, 0.0).astype(BF16)
        if b < 4:
            other = jnp.where(low, swap_halves(block), 0.0)
            q_ref[(2 * b + 1) * TOK : (2 * b + 2) * TOK, :] = other.astype(BF16)
    key = dot_nn(everyone, narrow[0:D, :])
    value = dot_nn(everyone, narrow[D : 2 * D, :])
    size = 4 * TOK
    first = rope(key[:, 0:LANES], cos, sin)
    kv_ref[0:size, :] = first.astype(BF16)
    kv_ref[size : 2 * size, :] = swap_halves(first).astype(BF16)
    kv_ref[2 * size : 3 * size, :] = rope(key[:, LANES:256], cos, sin).astype(BF16)
    kv_ref[3 * size : 4 * size, :] = value[:, 0:LANES].astype(BF16)
    kv_ref[4 * size : 5 * size, :] = swap_halves(value[:, 0:LANES]).astype(BF16)
    kv_ref[5 * size : 6 * size, :] = value[:, LANES:256].astype(BF16)
    heads = []
    for g in range(HK):
        keys, values = kv_of(kv_ref, g)
        rows = slice(3 * g * TOK, 3 * (g + 1) * TOK)
        scores = dot_nt(q_ref[rows, :], keys) * 0.125
        scores = jnp.where(visible, scores, MASKED)
        top = jnp.max(scores, -1, keepdims=True)
        weight = jnp.exp(scores - top)
        mass = jnp.sum(weight, -1, keepdims=True)
        total_ref[rows, :] = top + jnp.log(mass)
        probs = (weight * (1.0 / mass)).astype(BF16)
        out = dot_nn(probs, values)
        heads += [out[i * TOK : (i + 1) * TOK] for i in range(3)]
    mixed = merge_heads(heads).astype(BF16)
    early_ref[:, PAD : 2 * PAD] = mixed
    middle = own_stream + dot_nn(mixed[:, 0:D], matrix[D : 2 * D, 0:D])
    middle_ref[...] = middle
    recip = lax.rsqrt(jnp.mean(middle * middle, -1, keepdims=True) + EPSILON)
    early_ref[:, 2 * PAD :] = widen((middle * recip * gain_mid_ref[...]).astype(BF16))


def attend_fwd(batches, toks, gain, gain_mid, cos, sin, qpos, kpos):
    return pl.pallas_call(
        attend_kernel,
        out_shape=(
            shape((HQ * TOK, LANES), BF16),
            shape((24 * TOK, LANES), BF16),
            shape((TOK, 3 * PAD), BF16),
            shape((2 * D, PAD), BF16),
            shape((2 * D, 256), BF16),
            shape((HQ * TOK, 1), F32),
            shape((TOK, D), F32),
        ),
        in_specs=[any_spec()] * 30 + [vmem_spec()] * 10,
        out_specs=tuple([vmem_spec()] * 7),
        scratch_shapes=[
            pltpu.VMEM((6 * 96, LANES), BF16),
            pltpu.VMEM((2 * 288, LANES), BF16),
            pltpu.SemaphoreType.DMA((4,)),
        ],
        name="attend",
        compiler_params=pltpu.CompilerParams(vmem_limit_bytes=ROOM),
    )(*batches, *toks, gain, gain_mid, cos, sin, qpos, kpos)


def norm_back_block(gradient, stream, gain):
    recip = lax.rsqrt(jnp.mean(stream * stream, -1, keepdims=True) + EPSILON)
    unit = stream * recip
    gain_grad = jnp.sum(gradient * unit, 0, keepdims=True)
    scaled = gradient * gain
    back = recip * (scaled - unit * jnp.mean(scaled * unit, -1, keepdims=True))
    return back, gain_grad


def feed_kernel(*refs):
    batch = pairs_of(refs[:40])
    blocks = pairs_of(refs[40:80])
    (
        cot_ref, early_ref, middle_ref, gain_ref,
        out_ref, acts_ref, gmid_ref, gm_ref, gain_grad_ref,
        gate_w, up_w, down_w, half, act_keep, slope_keep, sems,
    ) = refs[80:]
    meta = coordinates()
    z = meta[0]
    for here, gate_from, up_from, down_from in (
        (0, 1, 2, 3),
        (1, 0, 3, 2),
        (2, 3, 0, 1),
        (3, 3, 1, 0),
    ):

        @pl.when(z == here)
        def _():
            fetch_wide(meta, blocks[gate_from], gate_w, sems.at[0])
            fetch_wide(meta, blocks[up_from], up_w, sems.at[1])
            fetch_down(meta, batch[down_from], down_w, half, sems.at[2], sems.at[3])

    grad_out = cot_ref[...].astype(F32).T
    grad_low = grad_out.astype(BF16)
    acts_ref[:, 3 * FF + PAD :] = widen(grad_low)
    nmid = early_ref[:, 2 * PAD : 2 * PAD + D]
    wait_all(gate_w, sems.at[0])
    wait_all(up_w, sems.at[1])
    span = 512
    for f in range(FF // span):
        part = slice(f * span, (f + 1) * span)
        gate = dot_nn(nmid, jnp.concatenate([gate_w[4 * f + n] for n in range(4)], 1))
        up = dot_nn(nmid, jnp.concatenate([up_w[4 * f + n] for n in range(4)], 1))
        sigma = jax.nn.sigmoid(gate)
        act = gate * sigma
        acts_ref[:, part] = (act * up).astype(BF16)
        act_keep[:, part] = act
        slope_keep[:, part] = up * sigma * (1.0 + gate * (1.0 - sigma))
    wait_all(down_w.at[:, 0:512], sems.at[2])
    wait_all(half, sems.at[3])
    place_halves(down_w, half, 8)
    result = middle_ref[...]
    dnorm = jnp.zeros((TOK, D), F32)
    for f in range(FF // span):
        part = slice(f * span, (f + 1) * span)
        gate_part = jnp.concatenate([gate_w[4 * f + n] for n in range(4)], 1)
        up_part = jnp.concatenate([up_w[4 * f + n] for n in range(4)], 1)
        result = result + dot_nn(acts_ref[:, part], down_w[part, 0:D])
        dhid = dot_nt(grad_low, down_w[part, 0:D])
        dgate = (dhid * slope_keep[:, part]).astype(BF16)
        dup = (dhid * act_keep[:, part]).astype(BF16)
        acts_ref[:, FF + f * span : FF + (f + 1) * span] = dgate
        acts_ref[:, 2 * FF + f * span : 2 * FF + (f + 1) * span] = dup
        dnorm = dnorm + dot_nt(dgate, gate_part) + dot_nt(dup, up_part)
    out_ref[...] = result.T
    back, gain_grad = norm_back_block(dnorm, middle_ref[...], gain_ref[...])
    gain_grad_ref[...] = gain_grad
    gmid = grad_out + back
    gmid_ref[...] = gmid
    gm = widen(gmid.astype(BF16))
    gm_ref[...] = gm
    acts_ref[:, 3 * FF : 3 * FF + PAD] = gm


ACTS = 3 * FF + 2 * PAD


def feed(batches, cotangent, early, middle, gain):
    views = [x.reshape(-1, 72, LANES) for x in batches]
    return pl.pallas_call(
        feed_kernel,
        out_shape=(
            shape((D, TOK), F32),
            shape((TOK, ACTS), BF16),
            shape((TOK, D), F32),
            shape((TOK, PAD), BF16),
            shape((1, D), F32),
        ),
        in_specs=[any_spec()] * 80 + [vmem_spec()] * 4,
        out_specs=tuple([vmem_spec()] * 5),
        scratch_shapes=[
            pltpu.VMEM((12, D, LANES), BF16),
            pltpu.VMEM((12, D, LANES), BF16),
            pltpu.VMEM((FF, PAD), BF16),
            pltpu.VMEM((8 * 96, LANES), BF16),
            pltpu.VMEM((TOK, FF), F32),
            pltpu.VMEM((TOK, FF), F32),
            pltpu.SemaphoreType.DMA((4,)),
        ],
        name="feed",
        compiler_params=pltpu.CompilerParams(vmem_limit_bytes=ROOM),
    )(*batches, *views, cotangent, early, middle, gain)


def store_tall(out_ref, row, product_):
    for c in range(4):
        out_ref[row + c * 192 : row + (c + 1) * 192, :] = product_[
            :, c * LANES : (c + 1) * LANES
        ].astype(BF16)
    half = product_[:, 512:PAD]
    low = lax.broadcasted_iota(jnp.int32, (96, LANES), 1) < 64
    packed = jnp.where(low, half[0:96], swap_halves(half[96:192]))
    out_ref[row + 768 : row + 864, :] = packed.astype(BF16)


def down_grads_kernel(
    acts0, acts1, after, out0, out1, out2, upper, lower, hid_t, last
):
    outs = (out0, out1, out2, last)
    _, core, place, _ = coordinates()
    for n, acts in enumerate((acts0, acts1)):
        part = acts[:, pl.ds(pl.multiple_of(core * 768, LANES), 768)]
        hid_t[:, n * TOK : (n + 1) * TOK] = part.astype(F32).T
    right = jnp.concatenate([acts0[:, 3 * FF + PAD :], acts1[:, 3 * FF + PAD :]], 0)
    left = jnp.concatenate(
        [hid_t[rows_at(lax.bitwise_xor(place, j) * 192, 192), :] for j in range(4)], 0
    ).astype(BF16)
    grad = dot_nn(left, right)
    for j in range(4):
        store_tall(outs[j], 0, grad[j * 192 : (j + 1) * 192, :])
    upper[...] = last[0:CUT, :]
    lower[...] = last[CUT:PIECE, :]


def down_grads(acts, acts_other, after):
    return pl.pallas_call(
        down_grads_kernel,
        out_shape=tuple([shape((PIECE, LANES), BF16)] * 3 + [shape((CUT, LANES), BF16)] * 2),
        in_specs=[vmem_spec()] * 2 + [any_spec()],
        out_specs=tuple([vmem_spec()] * 5),
        scratch_shapes=[pltpu.VMEM((768, 2 * TOK), F32), pltpu.VMEM((PIECE, LANES), BF16)],
        name="down_grads",
        compiler_params=pltpu.CompilerParams(vmem_limit_bytes=ROOM),
    )(acts, acts_other, after)


def gate_grads_kernel(
    early0, early1, acts0, acts1, after, out0, out1, out2, upper, lower, norm_t, stage
):
    outs = (out0, out1, out2)
    _, core, place, _ = coordinates()
    for n, early in enumerate((early0, early1)):
        norm_t[:, n * TOK : (n + 1) * TOK] = early[:, 2 * PAD :].astype(F32).T
    places = [lax.bitwise_xor(place, j) for j in range(4)]
    left = jnp.concatenate(
        [norm_t[rows_at(core * 288 + p * 72, 72), :] for p in places], 0
    ).astype(BF16)
    for n in range(2):
        columns = slice((n + 1) * FF, (n + 2) * FF)
        right = jnp.concatenate([acts0[:, columns], acts1[:, columns]], 0)
        grad = dot_nn(left, right)
        for j in range(4):
            for c in range(12):
                stage[c * 72 : (c + 1) * 72, :] = grad[
                    j * 72 : (j + 1) * 72, c * LANES : (c + 1) * LANES
                ]
            if j < 3:
                outs[j][n * PIECE : (n + 1) * PIECE, :] = stage[...].astype(BF16)
            else:
                (upper, lower)[n][...] = stage[...].astype(BF16)


def gate_grads(early, early_other, acts, acts_other, after):
    return pl.pallas_call(
        gate_grads_kernel,
        out_shape=tuple(
            [shape((2 * PIECE, LANES), BF16)] * 3 + [shape((PIECE, LANES), BF16)] * 2
        ),
        in_specs=[vmem_spec()] * 4 + [any_spec()],
        out_specs=tuple([vmem_spec()] * 5),
        scratch_shapes=[
            pltpu.VMEM((PAD, 2 * TOK), F32),
            pltpu.VMEM((PIECE, LANES), F32),
        ],
        name="gate_grads",
        compiler_params=pltpu.CompilerParams(vmem_limit_bytes=ROOM),
    )(early, early_other, acts, acts_other, after)


def attend_back_kernel(
    q_ref, kv_ref, qpos_ref, kpos_ref, total_ref, gm_ref, wo_ref, cos_ref, sin_ref,
    dq_ref, dkv0, dkv1, dkv2, dkv3,
):
    visible = kpos_ref[...] <= qpos_ref[...]
    visible = jnp.concatenate([visible] * 3, 0)
    low = lax.broadcasted_iota(jnp.int32, (TOK, LANES), 1) < 64
    dmix = dot_nt(gm_ref[:, 0:D], wo_ref[D : 2 * D, 0:D])
    dmix = widen(dmix)
    dheads = []
    for h in range(HQ):
        block = dmix[:, (h // 2) * LANES : (h // 2 + 1) * LANES]
        if h % 2:
            block = swap_halves(block)
        dheads.append(jnp.where(low, block, 0.0).astype(BF16))
    heads, dkeys, dvalues = [], [], []
    for g in range(HK):
        keys, values = kv_of(kv_ref, g)
        rows = slice(3 * g * TOK, 3 * (g + 1) * TOK)
        query = q_ref[rows, :]
        scores = dot_nt(query, keys) * 0.125
        probs = jnp.exp(jnp.where(visible, scores, MASKED) - total_ref[rows, :])
        dout = jnp.concatenate(dheads[3 * g : 3 * g + 3], 0)
        dprobs = dot_nt(dout, values)
        delta = jnp.sum(probs * dprobs, -1, keepdims=True)
        dscores = (probs * (dprobs - delta) * 0.125).astype(BF16)
        out = dot_nn(dscores, keys)
        heads += [out[i * TOK : (i + 1) * TOK] for i in range(3)]
        dkeys.append(dot_tn(dscores, query))
        dvalues.append(dot_tn(probs.astype(BF16), dout))
    dq = merge_heads(heads)
    cos = cos_ref[0:TOK, :]
    sin = sin_ref[0:TOK, :]
    for b in range(5):
        part = slice(b * LANES, (b + 1) * LANES)
        dq_ref[:, part] = unrope(dq[:, part], cos, sin).astype(BF16)
    for j, ref in enumerate((dkv0, dkv1, dkv2, dkv3)):
        rows = slice(j * TOK, (j + 1) * TOK)
        first = dkeys[0][rows] + swap_halves(dkeys[1][rows])
        middle = dkeys[2][rows] + swap_halves(dvalues[2][rows])
        last = dvalues[0][rows] + swap_halves(dvalues[1][rows])
        ref[0:TOK, :] = first.astype(BF16)
        ref[TOK : 2 * TOK, :] = middle.astype(BF16)
        ref[2 * TOK : 3 * TOK, :] = last.astype(BF16)


def attend_bwd(q, kv, qpos, kpos, total, gm, matrix, cos, sin):
    return pl.pallas_call(
        attend_back_kernel,
        out_shape=(shape((TOK, PAD), BF16),) + tuple([shape((3 * TOK, LANES), BF16)] * 4),
        in_specs=[vmem_spec()] * 9,
        out_specs=tuple([vmem_spec()] * 5),
        name="attend_back",
        compiler_params=pltpu.CompilerParams(vmem_limit_bytes=ROOM),
    )(q, kv, qpos, kpos, total, gm, matrix, cos, sin)


def input_kernel(
    dkv0, dkv1, dkv2, dkv3, dq_ref, gmid_ref, tok_ref, gain_ref, matrix, narrow, cos_ref, sin_ref,
    gain_mid_grad, after, grad_ref, dqkv_ref,
):
    total = (
        dkv0[...].astype(F32) + dkv1[...].astype(F32) + dkv2[...].astype(F32) + dkv3[...].astype(F32)
    )
    cos = cos_ref[0:TOK, :]
    sin = sin_ref[0:TOK, :]
    first = total[0:TOK]
    middle = total[TOK : 2 * TOK]
    last = total[2 * TOK : 3 * TOK]
    low = low_lanes(first)
    dk0 = unrope(first, cos, sin).astype(BF16)
    dk1 = jnp.where(low, unrope(middle, cos, sin), 0.0).astype(BF16)
    dv0 = last.astype(BF16)
    dv1 = jnp.where(low, swap_halves(middle), 0.0).astype(BF16)
    dkdv = jnp.concatenate([dk0, dk1, dv0, dv1], 1)
    dqkv_ref[0:TOK, 0:PAD] = dq_ref[...]
    dqkv_ref[0:TOK, PAD:] = dkdv
    d_in = (
        dot_nt(dq_ref[:, 0:D], matrix[0:D, 0:D])
        + dot_nt(dkdv[:, 0:256], narrow[0:D, :])
        + dot_nt(dkdv[:, 256:512], narrow[D : 2 * D, :])
    )
    back, gain_grad = norm_back_block(d_in, tok_ref[0:D, :].astype(F32).T, gain_ref[...])
    grad_ref[...] = (gmid_ref[...] + back).T
    rows = []
    for value in (gain_grad, gain_mid_grad[...]):
        rows += [value[:, n * LANES : (n + 1) * LANES] for n in range(4)]
        rows.append(jnp.concatenate([value[:, 512:576], jnp.zeros((1, 64), F32)], 1))
    gains = jnp.concatenate(rows + [jnp.zeros((6, LANES), F32)], 0)
    dqkv_ref[TOK : TOK + 32, 0:LANES] = split_rows(gains)
    dqkv_ref[TOK : TOK + 32, LANES:] = jnp.zeros((32, PAD + 512 - LANES), BF16)


def input_grads(dkvs, dq, gmid, tokens, gain, matrix, narrow, cos, sin, gain_mid_grad, after):
    return pl.pallas_call(
        input_kernel,
        out_shape=(shape((D, TOK), F32), shape((TOK + 32, PAD + 512), BF16)),
        in_specs=[vmem_spec()] * 13 + [any_spec()],
        out_specs=tuple([vmem_spec()] * 2),
        name="input_grads",
        compiler_params=pltpu.CompilerParams(vmem_limit_bytes=ROOM),
    )(*dkvs, dq, gmid, tokens, gain, matrix, narrow, cos, sin, gain_mid_grad, after)


def attend_grads_kernel(
    early0, early1, acts0, acts1, dqkv0, dqkv1,
    out0, out1, out2, out3, norm_t, left_t, pieces,
):
    _, core, place, _ = coordinates()
    for n, early in enumerate((early0, early1)):
        columns = slice(n * TOK, (n + 1) * TOK)
        turned = early[:, 0:PAD].astype(F32).T
        norm_t[:, columns] = turned.astype(BF16)

        @pl.when(core == 0)
        def _():
            left_t[:, columns] = turned.astype(BF16)

        @pl.when(core == 1)
        def _():
            left_t[:, columns] = early[:, PAD : 2 * PAD].astype(F32).T.astype(BF16)

    def tall(first, second):
        right = jnp.concatenate([first, second], 0)
        grad = dot_nn(left_t[0:D, :], right)
        for n in range(3):
            store_tall(pieces.at[n + core], 0, grad[n * 192 : (n + 1) * 192, :])

    def thin(first, second):
        right = jnp.concatenate([first, second], 0)
        grad = dot_nn(norm_t[0:D, :], right)
        ref = pieces.at[3 * (1 - core)]
        ref[0:D, :] = grad[:, 0:LANES].astype(BF16)
        half = grad[:, LANES:256]
        low = lax.broadcasted_iota(jnp.int32, (288, LANES), 1) < 64
        packed = jnp.where(low, half[0:288], swap_halves(half[288:576]))
        ref[D:PIECE, :] = packed.astype(BF16)

    @pl.when(core == 0)
    def _():
        tall(dqkv0[0:TOK, 0:PAD], dqkv1[0:TOK, 0:PAD])
        thin(dqkv0[0:TOK, PAD : PAD + 256], dqkv1[0:TOK, PAD : PAD + 256])

    @pl.when(core == 1)
    def _():
        tall(acts0[:, 3 * FF : 3 * FF + PAD], acts1[:, 3 * FF : 3 * FF + PAD])
        thin(dqkv0[0:TOK, PAD + 256 :], dqkv1[0:TOK, PAD + 256 :])

    gains = split_rows(unsplit(dqkv0.at[:, 0:LANES], TOK) + unsplit(dqkv1.at[:, 0:LANES], TOK))
    for j, out in enumerate((out0, out1, out2, out3)):
        out[0:PIECE, :] = pieces[lax.bitwise_xor(place, j)]
        out[PIECE : PIECE + 32, :] = gains


def attend_grads(*arrays):
    return pl.pallas_call(
        attend_grads_kernel,
        out_shape=tuple([shape((PIECE + 32, LANES), BF16)] * 4),
        in_specs=[vmem_spec()] * 6,
        out_specs=tuple([vmem_spec()] * 4),
        scratch_shapes=[
            pltpu.VMEM((PAD, 2 * TOK), BF16),
            pltpu.VMEM((PAD, 2 * TOK), BF16),
            pltpu.VMEM((4, PIECE, LANES), BF16),
        ],
        name="attend_grads",
        compiler_params=pltpu.CompilerParams(vmem_limit_bytes=ROOM),
    )(*arrays)


def fold_kernel(to_x, to_y, got_upper, got_lower, after, out_x, out_y):
    cut = got_upper.shape[0]
    out_x[0:cut, :] = to_x[0:cut, :]
    out_y[cut:, :] = to_y[cut:, :]
    out_x[cut:, :] = (to_x[cut:, :].astype(F32) + got_lower[...].astype(F32)).astype(BF16)
    out_y[0:cut, :] = (to_y[0:cut, :].astype(F32) + got_upper[...].astype(F32)).astype(BF16)


def fold(to_x, to_y, got_upper, got_lower, after):
    return pl.pallas_call(
        fold_kernel,
        out_shape=(shape(to_x.shape, BF16), shape(to_y.shape, BF16)),
        in_specs=[vmem_spec()] * 4 + [any_spec()],
        out_specs=(vmem_spec(), vmem_spec()),
        name="fold",
        compiler_params=pltpu.CompilerParams(vmem_limit_bytes=ROOM),
    )(to_x, to_y, got_upper, got_lower, after)


def down_sum_kernel(d0, d1, d2, out):
    total = d0[...].astype(F32) + d1[...].astype(F32) + d2[...].astype(F32)
    out[...] = total.astype(BF16)


def down_sum(parts):
    return pl.pallas_call(
        down_sum_kernel,
        out_shape=shape((PIECE, LANES), BF16),
        in_specs=[vmem_spec()] * 3,
        out_specs=vmem_spec(),
        name="down_sum",
        compiler_params=pltpu.CompilerParams(vmem_limit_bytes=ROOM),
    )(*parts)


def attend_sum_kernel(a0, a1, a2, a3, after, out, gain_out):
    attn = jnp.zeros((PIECE, LANES), F32)
    gains = jnp.zeros((16, LANES), F32)
    for part in (a0, a1, a2, a3):
        attn = attn + part[0:PIECE, :].astype(F32)
        gains = gains + unsplit(part, PIECE)
    out[...] = attn.astype(BF16)
    gain_out[...] = gains


def attend_sum(parts, after):
    return pl.pallas_call(
        attend_sum_kernel,
        out_shape=(shape((PIECE, LANES), BF16), shape((16, LANES), F32)),
        in_specs=[vmem_spec()] * 4 + [any_spec()],
        out_specs=(vmem_spec(), vmem_spec()),
        name="attend_sum",
        compiler_params=pltpu.CompilerParams(vmem_limit_bytes=ROOM),
    )(*parts, after)


def inner_kernel(g0, g1, g2, after, out1, out2, out3, base):
    z = coordinates()[0]
    total = g0[...].astype(F32) + g1[...].astype(F32) + g2[...].astype(F32)
    first, second = total[0:PIECE], total[PIECE:]
    for k, out in zip((1, 2, 3), (out1, out2, out3)):
        wanted = lax.bitwise_xor(z, k) == 1
        out[...] = jnp.where(wanted, first, second).astype(BF16)
    base[...] = jnp.where(z == 1, first, second)


def inner_planes(parts, after):
    piece = shape((PIECE, LANES), BF16)
    return pl.pallas_call(
        inner_kernel,
        out_shape=(piece, piece, piece, shape((PIECE, LANES), F32)),
        in_specs=[vmem_spec()] * 3 + [any_spec()],
        out_specs=tuple([vmem_spec()] * 4),
        name="inner",
        compiler_params=pltpu.CompilerParams(vmem_limit_bytes=ROOM),
    )(*parts, after)


def fast_shards(tokens, weights, gains, positions, cotangent):
    return fast_layer(tokens, weights, gains, positions, cotangent)


def fast_layer(tokens, weights, gains, positions, cotangent):
    z, _, _, _ = coordinates()

    def over_seq(array, j):
        return lax.ppermute(array, "seq", [(i, i ^ j) for i in range(4)])

    def over_dp(array, k, keep=lambda source, target: True):
        pairs = [(i, i ^ k) for i in range(8) if keep(i // 2, (i ^ k) // 2)]
        return lax.ppermute(array, "dp", pairs)

    own = prep(weights[0])
    from_z = [None] + [over_dp(own, 2 * k) for k in (1, 2, 3)]
    own_tok = extend(tokens[0].T, gains.reshape(1, 288), positions)
    toks = [own_tok] + [over_seq(own_tok, j) for j in (1, 2, 3)]
    cot = cotangent[0].T

    contents = [
        own,
        from_z[1],
        jnp.where(z == 3, from_z[3], from_z[2]),
        jnp.where(z == 3, from_z[2], from_z[3]),
    ]
    flat = []
    for content in contents:
        beside = over_seq(content, 1)
        across = over_seq(content, 2)
        upper, lower = split(beside, across)
        upper = over_seq(upper, 2)
        lower = over_seq(lower, 1)
        arrays = [content, beside, across, upper, lower]
        flat += arrays + [over_dp(x, 1) for x in arrays]

    half_width = HD // 2
    frequency = THETA_BASE ** (-((jnp.arange(LANES) % half_width).astype(F32) * (2.0 / HD)))
    gain_in, gain_mid, cos, sin, query_places, key_places = tables_of(toks, frequency[None])
    q, kv, early, matrix, narrow, total, middle = attend_fwd(
        flat[:30], toks, gain_in, gain_mid, cos, sin, query_places, key_places
    )
    early_other = over_dp(early, 1)
    result, acts, gmid, gm, gain_mid_grad = feed(flat, cot, early, middle, gain_mid)
    acts_other = over_dp(acts, 1)
    dq, *dkv_parts = attend_bwd(q, kv, query_places, key_places, total, gm, matrix, cos, sin)
    dkvs = [dkv_parts[0]] + [over_seq(dkv_parts[j], j) for j in (1, 2, 3)]

    def plane_step(parts):
        _, _, _, upper, lower = parts
        return [over_seq(upper, 1), over_seq(lower, 2)]

    def plane_finish(parts, got, after):
        own_part, to_x, to_y, _, _ = parts
        to_x, to_y = fold(to_x, to_y, *got, after)
        return [own_part, over_seq(to_x, 1), over_seq(to_y, 2)]

    down_parts = down_grads(acts, acts_other, dq)
    down_half = plane_step(down_parts)
    gate_parts = gate_grads(early, early_other, acts, acts_other, down_parts[0])
    gate_half = plane_step(gate_parts)
    input_grad, dqkv = input_grads(
        dkvs, dq, gmid, toks[0], gain_in, matrix, narrow, cos, sin, gain_mid_grad, gate_parts[3]
    )
    dqkv_other = over_dp(dqkv, 1)
    down_got = plane_finish(down_parts, down_half, dqkv)
    attend_parts = attend_grads(early, early_other, acts, acts_other, dqkv, dqkv_other)
    attend_got = [attend_parts[0]] + [over_seq(attend_parts[j], j) for j in (1, 2, 3)]

    gate_got = plane_finish(gate_parts, gate_half, attend_parts[0])

    def to_plane(array, plane):
        return [over_dp(array, 2 * k, lambda source, target: target == plane) for k in (1, 2, 3)]

    down_total = down_sum(down_got)
    from_planes = to_plane(down_total, 3)
    attend_total, gain_total = attend_sum(attend_got, down_total)
    from_planes += to_plane(attend_total, 0)
    gain_sums = [gain_total] + [over_dp(gain_total, 2 * k) for k in (1, 2, 3)]
    *inner_sums, inner_base = inner_planes(gate_got, attend_total)
    from_planes += [
        over_dp(inner_sums[k - 1], 2 * k, lambda source, target: target in (1, 2))
        for k in (1, 2, 3)
    ]
    gain_share = scales(gain_sums).reshape(288)
    weight_share = finish(attend_total, down_total, inner_base, from_planes, gain_share)
    return (result.T[None], input_grad.T[None], weight_share[None], gain_share)


def solution(mesh):
    timed = mesh.shape["dp"] == 8 and mesh.shape["seq"] == 4
    body = fast_shards if timed else shards
    return jax.shard_map(
        body,
        mesh=mesh,
        in_specs=(
            P("dp", "seq", None),
            P(None, ("dp", "seq"), None),
            P("seq"),
            P("dp", "seq"),
            P("dp", "seq", None),
        ),
        out_specs=(
            P("dp", "seq", None),
            P("dp", "seq", None),
            P(None, ("dp", "seq"), None),
            P("seq"),
        ),
        check_vma=False,
    )
```
